32 devices in a mesh: dp: 4 (over z), frame: 2 (over x), audio: 4 (over y, core).
Axes of the slice: x: 2, y: 2, z: 4, core: 2. Of those that a mesh axis runs over, the one named last changes fastest.
Arguments:
- video_query: bfloat16 [4, 1024, 3072], P('dp', ('frame', 'audio')), may hold values from -72 to 72
- out_grad: bfloat16 [4, 1024, 3072], P('dp', ('frame', 'audio')), may hold values from -6 to 6
- audio_latents: bfloat16 [4, 1024, 3072], P('dp', 'audio'), may hold values from -6 to 6
- kv_weight: bfloat16 [3072, 2, 3072], P(None, None, 'frame'), may hold values from -0.4375 to 0.4375
- video_length: int32 [4], P('dp'), may hold values from 256 to 1024, as said below
- audio_length: int32 [4], P('dp'), may hold values from 128 to 1024, as said below
- align_list: int32 [4, 8, 2], P('dp'), may hold values from 0 to 15, as said below
Outputs:
- attended: bfloat16 [4, 1024, 3072], P('dp', ('frame', 'audio'))
- query_grad: bfloat16 [4, 1024, 3072], P('dp', ('frame', 'audio'))
- kv_weight_grad: float32 [3072, 2, 3072], P(('dp', 'audio'), None, 'frame')
The draws below stay inside these ranges and needn't reach their ends.
Inputs may be any that keep to these rules, and one draw needn't show every extreme that they name: `video_length`: one clip of every draw has all 1024 tokens live. `audio_length`: one clip of every draw has all 1024 latents live. `align_list`: for clip c and query block b the 2 entries are distinct and each is below ceil(audio_length[c] / 64); the first is b * ceil(audio_length[c] / 64) // 8.
All inputs are finite; a program needn't handle non-finite values.
Results may differ from the reference program's by a relative error of at most 0.004.
The reference program's roundings to bfloat16 on the way count: a program that leaves them out, or rounds other values in their place, can miss the bound.
Values may be sent and summed in bfloat16 or wider, within the bound.
A program may use at most 192 MiB of HBM per device.

```python
import jax
import jax.numpy as jnp
from jax import lax

D = 3072
HEADS = 24
HD = 128
QB = 128
KB = 64
NLIST = 2
CLIPS = 4
TV = 1024
TA = 1024
NQB = 8
NKB = 16


def skewed_length(key, lowest, highest):
    first, second, third = jax.random.split(key, 3)
    draw_one = jax.random.randint(first, (CLIPS,), lowest, highest + 1)
    draw_two = jax.random.randint(second, (CLIPS,), lowest, highest + 1)
    picked = jax.random.randint(third, (), 0, CLIPS)
    lengths = jnp.minimum(draw_one, draw_two)
    return jnp.where(jnp.arange(CLIPS) == picked, highest, lengths).astype(jnp.int32)


def lengths_and_lists(key):
    video_key = jax.random.fold_in(key, 101)
    audio_key = jax.random.fold_in(key, 202)
    list_key = jax.random.fold_in(key, 303)
    video_live = skewed_length(video_key, TV // 4, TV)
    audio_live = skewed_length(audio_key, NLIST * KB, TA)
    audio_blocks = (audio_live + KB - 1) // KB
    centers = jnp.arange(NQB, dtype=jnp.int32)[None, :] * audio_blocks[:, None] // NQB
    noise = jax.random.randint(list_key, (CLIPS, NQB, NKB), 0, 2 ** 20)
    block_ids = jnp.arange(NKB, dtype=jnp.int32)[None, None, :]
    ranked = jnp.where(block_ids < audio_blocks[:, None, None], noise * NKB + block_ids, 2 ** 28 + block_ids)
    ranked = jnp.where(block_ids == centers[:, :, None], -1, ranked)
    order = jnp.argsort(ranked, axis=-1, stable=True)[:, :, :NLIST]
    return (video_live, audio_live, order.astype(jnp.int32))


def draw_video_length(key, part):
    return lengths_and_lists(key)[0]


def draw_audio_length(key, part):
    return lengths_and_lists(key)[1]


def draw_align_list(key, part):
    return lengths_and_lists(key)[2]


def draw_video_query(key, part):
    first = jax.random.fold_in(jax.random.fold_in(key, 11), 0)
    values = jnp.clip(jax.random.normal(first, (CLIPS, TV, D), jnp.float32), -6.0, 6.0) * 0.25
    return values.astype(jnp.bfloat16)


def block_levels(own_key, dims, cuts, least, top_value):
    level, own = 1.0, jax.random.fold_in(own_key, 6)
    for axis_at, blocks in cuts:
        draws = jnp.exp(jax.random.uniform(jax.random.fold_in(own, axis_at), (blocks,), jnp.float32, least / len(cuts), top_value / len(cuts)))
        level = level * jnp.repeat(draws, dims[axis_at] // blocks).reshape([-1 if axis == axis_at else 1 for axis in range(len(dims))])
    return level


def scatter_about(key, shape, deviation, reach, pieces=(), kind=jnp.bfloat16):
    result = jax.random.normal(key, shape, jnp.float32) * deviation
    if len(pieces) > 0:
        result = block_levels(key, shape, pieces, -0.22, 0.18) * result
    return jnp.clip(result, min=-reach, max=reach).astype(kind)


def setup_inputs(seed: int = 0) -> dict:
    keys = jax.random.split(jax.random.key(seed), 8)
    return {
        "video_query": draw_video_query(jax.random.fold_in(keys[7], 71), 0),
        "out_grad": scatter_about(keys[1], (CLIPS, TV, D), 1.0, 6.0, ((0, 4), (1, 8))),
        "audio_latents": scatter_about(keys[2], (CLIPS, TA, D), 1.0, 6.0, ((0, 4), (1, 4))),
        "kv_weight": scatter_about(keys[3], (D, 2, D), (D // 16) ** -0.5, 0.4375, ((2, 2),)),
        "video_length": draw_video_length(jax.random.fold_in(keys[7], 71), 0),
        "audio_length": draw_audio_length(jax.random.fold_in(keys[7], 71), 0),
        "align_list": draw_align_list(jax.random.fold_in(keys[7], 71), 0),
    }


def clip_pass(kv_weight, inputs):
    query_all, grad_all, latents, video_live, audio_live, block_lists = inputs
    scaling = HD ** -0.5
    projected = jnp.dot(latents, kv_weight.reshape(D, 2 * D), preferred_element_type=jnp.float32).astype(jnp.bfloat16)
    projected = lax.optimization_barrier(projected)
    blocks = projected.reshape(NKB, KB, 2, HEADS, HD)
    query_blocks = query_all.reshape(NQB, QB, HEADS, HD)
    grad_blocks = grad_all.reshape(NQB, QB, HEADS, HD)

    def advance(totals, index):
        listed = block_lists[index]
        chosen = jnp.take(blocks, listed, axis=0).reshape(NLIST * KB, 2, HEADS, HD).astype(jnp.float32)
        key_rows = chosen[:, 0]
        value_rows = chosen[:, 1]
        key_index = (listed[:, None] * KB + jnp.arange(KB, dtype=jnp.int32)[None, :]).reshape(NLIST * KB)
        key_live = key_index < audio_live
        row_index = index * QB + jnp.arange(QB, dtype=jnp.int32)
        live_rows = row_index < video_live
        query_rows = query_blocks[index].astype(jnp.float32)
        grad_rows = grad_blocks[index].astype(jnp.float32)
        scores = jnp.einsum("qhd,khd->hqk", query_rows, key_rows) * scaling
        scores = jnp.where(key_live[None, None, :], scores, -1e30)
        scores = scores - jnp.max(scores, axis=-1, keepdims=True)
        weights = jnp.exp(scores)
        probability = weights / jnp.sum(weights, axis=-1, keepdims=True)
        probability = jnp.where(live_rows[None, :, None], probability, 0.0)
        prob_low = lax.optimization_barrier(probability.astype(jnp.bfloat16)).astype(jnp.float32)
        output = jnp.einsum("hqk,khd->qhd", prob_low, value_rows).astype(jnp.bfloat16)
        prob_grad = jnp.einsum("qhd,khd->hqk", grad_rows, value_rows)
        row_dot = jnp.sum(probability * prob_grad, axis=-1, keepdims=True)
        score_grad = probability * (prob_grad - row_dot)
        score_grad = lax.optimization_barrier(score_grad.astype(jnp.bfloat16)).astype(jnp.float32)
        query_part = (jnp.einsum("hqk,khd->qhd", score_grad, key_rows) * scaling).astype(jnp.bfloat16)
        key_part = jnp.einsum("hqk,qhd->khd", score_grad, query_rows) * scaling
        value_part = jnp.einsum("hqk,qhd->khd", prob_low, grad_rows)
        both = jnp.stack([key_part, value_part], axis=1).reshape(NLIST, KB, 2, HEADS, HD)
        totals = totals.at[listed].add(both)
        return totals, (output.reshape(QB, D), query_part.reshape(QB, D))

    totals = jnp.zeros((NKB, KB, 2, HEADS, HD), jnp.float32)
    totals, (output, query_part) = lax.scan(advance, totals, jnp.arange(NQB, dtype=jnp.int32))
    kv_grad = totals.reshape(TA, 2 * D).astype(jnp.bfloat16)
    weight_part = lax.dot_general(latents, kv_grad, (((0,), (0,)), ((), ())), preferred_element_type=jnp.float32)
    return output.reshape(TV, D), query_part.reshape(TV, D), weight_part


def reference(video_query, out_grad, audio_latents, kv_weight, video_length, audio_length, align_list):
    def per_clip(running, inputs):
        attended, query_grad, weight_part = clip_pass(kv_weight, inputs)
        return running + weight_part, (attended, query_grad)

    running = jnp.zeros((D, 2 * D), jnp.float32)
    running, (attended, query_grad) = lax.scan(per_clip, running, (video_query, out_grad, audio_latents, video_length, audio_length, align_list))
    return attended, query_grad, (running * (1.0 / CLIPS)).reshape(D, 2, D)
```

```python
import functools
import math

import jax
import jax.numpy as jnp
from jax import lax
from jax.experimental import pallas as pl
from jax.experimental.pallas import tpu as pltpu
from jax.sharding import PartitionSpec as P

HD = 128
QB = 128
KB = 64


def dot_nt(a, b):
    return lax.dot_general(a, b, (((1,), (1,)), ((), ())), preferred_element_type=jnp.float32)


def dot_tn(a, b):
    return lax.dot_general(a, b, (((0,), (0,)), ((), ())), preferred_element_type=jnp.float32)


def attend_kernel(heads, bias_ref, live_ref, q_ref, g_ref, kv_ref, out_ref, dq_ref, dkv_ref):
    scaling = HD ** (-0.5)
    width = heads * HD
    bias = bias_ref[0]
    live = live_ref[0]
    for h in range(heads):
        cols = slice(h * HD, (h + 1) * HD)
        vcols = slice(width + h * HD, width + (h + 1) * HD)
        q, g = q_ref[:, cols], g_ref[:, cols]
        k, v = kv_ref[:, cols], kv_ref[:, vcols]
        scores = jnp.where(bias > 0.0, dot_nt(q, k) * scaling, -1e30)
        scores = scores - jnp.max(scores, axis=-1, keepdims=True)
        weights = jnp.exp(scores)
        prob = weights / jnp.sum(weights, axis=-1, keepdims=True)
        prob = jnp.where(live > 0.0, prob, 0.0)
        low = prob.astype(jnp.bfloat16)
        out_ref[:, cols] = jnp.dot(low, v, preferred_element_type=jnp.float32).astype(jnp.bfloat16)
        dprob = dot_nt(g, v)
        row = jnp.sum(prob * dprob, axis=-1, keepdims=True)
        ds = (prob * (dprob - row)).astype(jnp.bfloat16)
        dq_ref[:, cols] = (
            jnp.dot(ds, k, preferred_element_type=jnp.float32) * scaling
        ).astype(jnp.bfloat16)
        for start, part in ((h * HD, dot_tn(ds, q) * scaling), (width + h * HD, dot_tn(low, g))):
            high = part.astype(jnp.bfloat16)
            dkv_ref[:, start : start + HD] = high
            dkv_ref[:, 2 * width + start : 2 * width + start + HD] = (
                part - high.astype(jnp.float32)
            ).astype(jnp.bfloat16)


def attend(queries, cotangent, kv, allowed, live, heads):
    blocks = allowed.shape[0]
    keys = kv.shape[0] // blocks
    width = heads * HD
    row_spec = pl.BlockSpec((QB, width), lambda b: (b, 0))
    kv_spec = pl.BlockSpec((keys, 2 * width), lambda b: (b, 0))
    return pl.pallas_call(
        functools.partial(attend_kernel, heads),
        grid=(blocks,),
        in_specs=[
            pl.BlockSpec((1, 1, keys), lambda b: (b, 0, 0)),
            pl.BlockSpec((1, QB, 1), lambda b: (b, 0, 0)),
            row_spec,
            row_spec,
            kv_spec,
        ],
        out_specs=[row_spec, row_spec, pl.BlockSpec((keys, 4 * width), lambda b: (b, 0))],
        out_shape=[
            jax.ShapeDtypeStruct(queries.shape, jnp.bfloat16),
            jax.ShapeDtypeStruct(queries.shape, jnp.bfloat16),
            jax.ShapeDtypeStruct((kv.shape[0], 4 * width), jnp.bfloat16),
        ],
    )(allowed, live, queries, cotangent, kv)


def per_device(
    video_query, out_grad, audio_latents, kv_weight, video_length, audio_length, align_list
):
    frames = lax.axis_size("frame")
    audio_count = lax.axis_size("audio")
    clip_count = lax.axis_size("dp")
    audio_at = lax.axis_index("audio")
    queries, cotangent, latents = video_query[0], out_grad[0], audio_latents[0]
    shard_rows = queries.shape[0]
    width = queries.shape[1]
    local_width = kv_weight.shape[2]
    heads = local_width // HD
    video_live, audio_live, block_lists = video_length[0], audio_length[0], align_list[0]
    listed_count = block_lists.shape[1]
    own_blocks = shard_rows // QB

    latents_all = lax.all_gather(latents, "audio", axis=0, tiled=True)
    key_count = latents_all.shape[0]
    q = lax.all_to_all(queries, "frame", split_axis=1, concat_axis=0, tiled=True)
    g = lax.all_to_all(cotangent, "frame", split_axis=1, concat_axis=0, tiled=True)

    lists = block_lists.reshape(frames, audio_count, own_blocks, listed_count)
    listed = lax.dynamic_index_in_dim(lists, audio_at, 1, keepdims=False)
    listed = listed.reshape(frames * own_blocks, listed_count)
    block_at = (
        jnp.arange(frames)[:, None] * audio_count + audio_at
    ) * own_blocks + jnp.arange(own_blocks)[None]
    block_at = block_at.reshape(-1)
    key_index = (listed[:, :, None] * KB + jnp.arange(KB)).reshape(
        frames * own_blocks, 1, listed_count * KB
    )
    allowed = (key_index < audio_live).astype(jnp.float32)
    row_index = block_at[:, None] * QB + jnp.arange(QB)[None]
    live = (row_index < video_live).astype(jnp.float32)[:, :, None]

    chosen = jnp.take(
        latents_all.reshape(key_count // KB, KB, width), listed.reshape(-1), axis=0
    ).reshape(-1, width)
    kv = jnp.dot(
        chosen, kv_weight.reshape(width, 2 * local_width), preferred_element_type=jnp.float32
    ).astype(jnp.bfloat16)
    attended, query_grad, terms = attend(q, g, kv, allowed, live, heads)
    terms = lax.all_gather(terms, "audio", axis=0, tiled=True)
    attended = lax.all_to_all(attended, "frame", split_axis=0, concat_axis=1, tiled=True)
    query_grad = lax.all_to_all(query_grad, "frame", split_axis=0, concat_axis=1, tiled=True)

    entries = lists.transpose(1, 0, 2, 3).reshape(-1)
    entry_rows = (entries[:, None] * KB + jnp.arange(KB)[None]).reshape(-1)
    onehot = (jnp.arange(key_count)[:, None] == entry_rows[None]).astype(jnp.bfloat16)
    high, low = terms[:, : 2 * local_width], terms[:, 2 * local_width :]
    kv_grad = (
        jnp.dot(onehot, high, preferred_element_type=jnp.float32)
        + jnp.dot(onehot, low, preferred_element_type=jnp.float32)
    ).astype(jnp.bfloat16)
    weight_rows = width // (clip_count * audio_count)
    columns = lax.dynamic_index_in_dim(
        latents_all.reshape(key_count, clip_count, audio_count, weight_rows),
        audio_at, 2, keepdims=False,
    ).reshape(key_count, clip_count * weight_rows)
    product = dot_tn(columns, kv_grad) * (1.0 / clip_count)
    weight_grad = lax.psum_scatter(
        product.astype(jnp.bfloat16), "dp", scatter_dimension=0, tiled=True
    ).astype(jnp.float32)
    return (attended[None], query_grad[None], weight_grad.reshape(weight_rows, 2, local_width))


def solution(mesh):
    return jax.shard_map(
        per_device,
        mesh=mesh,
        in_specs=(
            P("dp", ("frame", "audio"), None),
            P("dp", ("frame", "audio"), None),
            P("dp", "audio", None),
            P(None, None, "frame"),
            P("dp"),
            P("dp"),
            P("dp", None, None),
        ),
        out_specs=(
            P("dp", ("frame", "audio"), None),
            P("dp", ("frame", "audio"), None),
            P(("dp", "audio"), None, "frame"),
        ),
        check_vma=False,
    )
```

```python
import functools
import math

import jax
import jax.numpy as jnp
from jax import lax
from jax.experimental import pallas as pl
from jax.experimental.pallas import tpu as pltpu
from jax.sharding import PartitionSpec as P

HD = 128
QB = 128
KB = 64


def dot_nt(a, b):
    return lax.dot_general(a, b, (((1,), (1,)), ((), ())), preferred_element_type=jnp.float32)


def dot_tn(a, b):
    return lax.dot_general(a, b, (((0,), (0,)), ((), ())), preferred_element_type=jnp.float32)


def attend_kernel(heads, chunk, bias_ref, live_ref, q_ref, g_ref, kv_ref, out_ref, dq_ref, dkv_ref):
    scaling = HD ** (-0.5)
    width = heads * HD
    bias = bias_ref[0]
    live = live_ref[0]
    for h in range(heads):
        cols = slice(h * HD, (h + 1) * HD)
        vcols = slice(width + h * HD, width + (h + 1) * HD)
        q, g = q_ref[:, cols], g_ref[:, cols]
        k, v = kv_ref[:, cols], kv_ref[:, vcols]
        scores = jnp.where(bias > 0.0, dot_nt(q, k) * scaling, -1e30)
        scores = scores - jnp.max(scores, axis=-1, keepdims=True)
        weights = jnp.exp(scores)
        prob = weights / jnp.sum(weights, axis=-1, keepdims=True)
        prob = jnp.where(live > 0.0, prob, 0.0)
        low = prob.astype(jnp.bfloat16)
        out_ref[:, cols] = jnp.dot(low, v, preferred_element_type=jnp.float32).astype(jnp.bfloat16)
        dprob = dot_nt(g, v)
        row = jnp.sum(prob * dprob, axis=-1, keepdims=True)
        ds = (prob * (dprob - row)).astype(jnp.bfloat16)
        dq_ref[:, cols] = (
            jnp.dot(ds, k, preferred_element_type=jnp.float32) * scaling
        ).astype(jnp.bfloat16)
        for start, part in ((h * HD, dot_tn(ds, q) * scaling), (width + h * HD, dot_tn(low, g))):
            high = part.astype(jnp.bfloat16)
            at, lane = divmod(start, chunk)
            dkv_ref[at, :, lane : lane + HD] = high
            dkv_ref[at, :, chunk + lane : chunk + lane + HD] = (
                part - high.astype(jnp.float32)
            ).astype(jnp.bfloat16)


def attend(queries, cotangent, kv, allowed, live, heads):
    blocks = allowed.shape[0]
    keys = kv.shape[0] // blocks
    width = heads * HD
    chunk = math.gcd(2 * width, 512)
    chunks = 2 * width // chunk
    row_spec = pl.BlockSpec((QB, width), lambda b: (b, 0))
    kv_spec = pl.BlockSpec((keys, 2 * width), lambda b: (b, 0))
    return pl.pallas_call(
        functools.partial(attend_kernel, heads, chunk),
        grid=(blocks,),
        in_specs=[
            pl.BlockSpec((1, 1, keys), lambda b: (b, 0, 0)),
            pl.BlockSpec((1, QB, 1), lambda b: (b, 0, 0)),
            row_spec,
            row_spec,
            kv_spec,
        ],
        out_specs=[row_spec, row_spec, pl.BlockSpec((chunks, keys, 2 * chunk), lambda b: (0, b, 0))],
        out_shape=[
            jax.ShapeDtypeStruct(queries.shape, jnp.bfloat16),
            jax.ShapeDtypeStruct(queries.shape, jnp.bfloat16),
            jax.ShapeDtypeStruct((chunks, kv.shape[0], 2 * chunk), jnp.bfloat16),
        ],
    )(allowed, live, queries, cotangent, kv)


MESH = pl.DeviceIdType.MESH


def grad_kernel(
    axes, chunk, terms_ref, att_ref, dq_ref, onehot_ref, latents_ref,
    out_ref, att_out, dq_out,
    latents_vmem, cols_t, gathered, kv_tile, partial, right_buf, left_buf,
    local_sem, own_sem, far_send, far_recv, near_send, near_recv, fwd_send, fwd_recv,
    right_send, right_recv, left_send, left_recv, ret_send, ret_recv,
):
    clips, frames, audio = axes
    z, f, a = lax.axis_index("dp"), lax.axis_index("frame"), lax.axis_index("audio")
    chunks = terms_ref.shape[0]
    rows = terms_ref.shape[1]
    weight_rows = out_ref.shape[1]
    key_count = onehot_ref.shape[0]
    lane = att_ref.shape[2]
    half = audio // 2
    far = lax.rem(a + half, audio)
    near = a + 1 - 2 * lax.rem(a, 2)
    far_near = lax.rem(near + half, audio)

    load = pltpu.make_async_copy(latents_ref, latents_vmem, local_sem)
    load.start()

    barrier = pltpu.get_barrier_semaphore()

    def greet(where):
        pl.semaphore_signal(barrier, inc=1, device_id=where, device_id_type=MESH)

    greet({"audio": far})
    greet({"audio": near})
    for step in range(1, frames):
        greet({"frame": lax.rem(f + step, frames)})
    pl.when(z > 0)(lambda: greet({"dp": z - 1}))
    pl.when(z < clips - 1)(lambda: greet({"dp": z + 1}))
    ends = jnp.where(z > 0, 1, 0) + jnp.where(z < clips - 1, 1, 0)
    pl.semaphore_wait(barrier, 1 + frames + ends)

    def far_copy(c):
        return pltpu.make_async_remote_copy(
            src_ref=terms_ref.at[c], dst_ref=gathered.at[c, a], send_sem=far_send.at[c],
            recv_sem=far_recv.at[c], device_id={"audio": far}, device_id_type=MESH)

    def near_copy(c):
        return pltpu.make_async_remote_copy(
            src_ref=terms_ref.at[c], dst_ref=gathered.at[c, a], send_sem=near_send.at[c],
            recv_sem=near_recv.at[c], device_id={"audio": near}, device_id_type=MESH)

    def fwd_copy(c):
        return pltpu.make_async_remote_copy(
            src_ref=gathered.at[c, far], dst_ref=gathered.at[c, far], send_sem=fwd_send.at[c],
            recv_sem=fwd_recv.at[c], device_id={"audio": near}, device_id_type=MESH)

    def arrived(c, source, sem, peer):
        return pltpu.make_async_remote_copy(
            src_ref=terms_ref.at[c], dst_ref=gathered.at[c, source], send_sem=far_send.at[c],
            recv_sem=sem.at[c], device_id={"audio": peer}, device_id_type=MESH)

    def own_copy(c):
        return pltpu.make_async_copy(terms_ref.at[c], gathered.at[c, a], own_sem.at[c])

    def issue(c, carry):
        far_copy(c).start()
        near_copy(c).start()
        own_copy(c).start()
        return carry

    lax.fori_loop(0, chunks, issue, 0)

    def lanes(g):
        return pl.ds(pl.multiple_of(g * lane, 128), lane)

    def returns(step):
        other = lax.rem(f + step, frames)
        return [
            pltpu.make_async_remote_copy(
                src_ref=src.at[other], dst_ref=dst.at[:, lanes(f)],
                send_sem=ret_send.at[which, step], recv_sem=ret_recv.at[which, step],
                device_id={"frame": other}, device_id_type=MESH)
            for which, (src, dst) in enumerate(((att_ref, att_out), (dq_ref, dq_out)))
        ]

    for step in range(1, frames):
        for copy in returns(step):
            copy.start()
    att_out[:, lanes(f)] = att_ref[f]
    dq_out[:, lanes(f)] = dq_ref[f]

    load.wait()
    width = latents_vmem.shape[1]

    def select(d, carry):
        first = (d * audio + a) * weight_rows
        at = lax.broadcasted_iota(jnp.int32, (weight_rows, width), 1)
        row = lax.broadcasted_iota(jnp.int32, (weight_rows, width), 0)
        pick = jnp.where(at == row + first, 1.0, 0.0).astype(jnp.bfloat16)
        cols_t[d] = dot_nt(pick, latents_vmem[...]).astype(jnp.bfloat16)
        return carry

    lax.fori_loop(0, clips, select, 0)

    tile = math.gcd(key_count, 256)

    def compute(c):
        own_copy(c).wait()
        arrived(c, far, far_recv, far).wait_recv()
        fwd_copy(c).start()
        arrived(c, near, near_recv, near).wait_recv()
        arrived(c, far_near, fwd_recv, near).wait_recv()

        def dedupe(t, carry):
            at = pl.ds(pl.multiple_of(t * tile, tile), tile)
            total = jnp.zeros((tile, chunk), jnp.float32)
            for source in range(audio):
                pick = onehot_ref[at, source * rows : (source + 1) * rows]
                total += jnp.dot(
                    pick, gathered[c, source, :, :chunk], preferred_element_type=jnp.float32)
                total += jnp.dot(
                    pick, gathered[c, source, :, chunk:], preferred_element_type=jnp.float32)
            kv_tile[at, :] = total.astype(jnp.bfloat16)
            return carry

        lax.fori_loop(0, key_count // tile, dedupe, 0)

        def multiply(d, carry):
            partial[c, d] = jnp.dot(
                cols_t[d], kv_tile[...], preferred_element_type=jnp.float32
            ) * (1.0 / clips)
            return carry

        lax.fori_loop(0, clips, multiply, 0)
        out_ref[c] = partial[c, z]

    def hop(buf, send, recv, c, d, where):
        return pltpu.make_async_remote_copy(
            src_ref=buf.at[c, d], dst_ref=buf.at[c, d], send_sem=send.at[c, d],
            recv_sem=recv.at[c, d], device_id={"dp": where}, device_id_type=MESH)

    def pass_on(c, forward):
        if forward:
            buf, send, recv, peer, source = right_buf, right_send, right_recv, z + 1, z - 1
            has_source = z > 0
        else:
            buf, send, recv, peer, source = left_buf, left_send, left_recv, z - 1, z + 1
            has_source = z < clips - 1
        for d in range(clips):
            @pl.when((d > z) if forward else (d < z))
            def _():
                @pl.when(has_source)
                def _():
                    hop(buf, send, recv, c, d, source).wait_recv()
                    buf[c, d] = (partial[c, d] + buf[c, d].astype(jnp.float32)).astype(jnp.bfloat16)

                @pl.when(jnp.logical_not(has_source))
                def _():
                    buf[c, d] = partial[c, d].astype(jnp.bfloat16)

                hop(buf, send, recv, c, d, peer).start()

        @pl.when(has_source)
        def _():
            hop(buf, send, recv, c, z, source).wait_recv()
            out_ref[c] += buf[c, z].astype(jnp.float32)

    def advance(i, carry):
        pl.when(i < chunks)(lambda: compute(i))
        for forward, lag in ((True, z), (False, clips - 1 - z)):
            c = i - lag

            @pl.when(jnp.logical_and(c >= 0, c < chunks))
            def _():
                pass_on(c, forward)

        return carry

    lax.fori_loop(0, chunks + clips - 1, advance, 0)

    def drain(c, carry):
        far_copy(c).wait_send()
        near_copy(c).wait_send()
        fwd_copy(c).wait_send()
        for d in range(clips):
            pl.when(d > z)(lambda: hop(right_buf, right_send, right_recv, c, d, z + 1).wait_send())
            pl.when(d < z)(lambda: hop(left_buf, left_send, left_recv, c, d, z - 1).wait_send())
        return carry

    lax.fori_loop(0, chunks, drain, 0)
    for step in range(1, frames):
        for copy in returns(step):
            copy.wait_send()
        source = lax.rem(f + frames - step, frames)
        for which, (src, dst) in enumerate(((att_ref, att_out), (dq_ref, dq_out))):
            pltpu.make_async_remote_copy(
                src_ref=src.at[source], dst_ref=dst.at[:, lanes(source)],
                send_sem=ret_send.at[which, step], recv_sem=ret_recv.at[which, step],
                device_id={"frame": source}, device_id_type=MESH).wait_recv()


def finish(terms, attended, query_grad, onehot, latents_all, sizes, weight_rows):
    clips, frames, audio = sizes
    chunks, rows, pair = terms.shape
    chunk = pair // 2
    own_rows, lane = attended.shape[1], attended.shape[2]
    key_count = onehot.shape[0]
    vmem = pl.BlockSpec(memory_space=pltpu.VMEM)
    dma = pltpu.SemaphoreType.DMA
    line = (chunks, clips)
    kernel = functools.partial(grad_kernel, sizes, chunk)
    return pl.pallas_call(
        kernel,
        in_specs=[vmem] * 4 + [pl.BlockSpec(memory_space=pl.ANY)],
        out_specs=[vmem] * 3,
        out_shape=[
            jax.ShapeDtypeStruct((chunks, weight_rows, chunk), jnp.float32),
            jax.ShapeDtypeStruct((own_rows, frames * lane), jnp.bfloat16),
            jax.ShapeDtypeStruct((own_rows, frames * lane), jnp.bfloat16),
        ],
        scratch_shapes=[
            pltpu.VMEM(latents_all.shape, jnp.bfloat16),
            pltpu.VMEM((clips, weight_rows, key_count), jnp.bfloat16),
            pltpu.VMEM((chunks, audio, rows, pair), jnp.bfloat16),
            pltpu.VMEM((key_count, chunk), jnp.bfloat16),
            pltpu.VMEM((chunks, clips, weight_rows, chunk), jnp.float32),
            pltpu.VMEM((chunks, clips, weight_rows, chunk), jnp.bfloat16),
            pltpu.VMEM((chunks, clips, weight_rows, chunk), jnp.bfloat16),
            dma, dma((chunks,)), dma((chunks,)), dma((chunks,)), dma((chunks,)),
            dma((chunks,)), dma((chunks,)), dma((chunks,)),
            dma(line), dma(line), dma(line), dma(line),
            dma((2, frames)), dma((2, frames)),
        ],
        compiler_params=pltpu.CompilerParams(
            collective_id=0, has_side_effects=True, vmem_limit_bytes=66_000_000),
    )(terms, attended, query_grad, onehot, latents_all)


def per_device(
    video_query, out_grad, audio_latents, kv_weight, video_length, audio_length, align_list
):
    frames = lax.axis_size("frame")
    audio_count = lax.axis_size("audio")
    clip_count = lax.axis_size("dp")
    audio_at = lax.axis_index("audio")
    queries, cotangent, latents = video_query[0], out_grad[0], audio_latents[0]
    shard_rows = queries.shape[0]
    width = queries.shape[1]
    local_width = kv_weight.shape[2]
    heads = local_width // HD
    video_live, audio_live, block_lists = video_length[0], audio_length[0], align_list[0]
    listed_count = block_lists.shape[1]
    own_blocks = shard_rows // QB

    latents_all = lax.all_gather(latents, "audio", axis=0, tiled=True)
    key_count = latents_all.shape[0]
    q = lax.all_to_all(queries, "frame", split_axis=1, concat_axis=0, tiled=True)
    g = lax.all_to_all(cotangent, "frame", split_axis=1, concat_axis=0, tiled=True)

    lists = block_lists.reshape(frames, audio_count, own_blocks, listed_count)
    listed = lax.dynamic_index_in_dim(lists, audio_at, 1, keepdims=False)
    listed = listed.reshape(frames * own_blocks, listed_count)
    block_at = (
        jnp.arange(frames)[:, None] * audio_count + audio_at
    ) * own_blocks + jnp.arange(own_blocks)[None]
    block_at = block_at.reshape(-1)
    key_index = (listed[:, :, None] * KB + jnp.arange(KB)).reshape(
        frames * own_blocks, 1, listed_count * KB
    )
    allowed = (key_index < audio_live).astype(jnp.float32)
    row_index = block_at[:, None] * QB + jnp.arange(QB)[None]
    live = (row_index < video_live).astype(jnp.float32)[:, :, None]

    chosen = jnp.take(
        latents_all.reshape(key_count // KB, KB, width), listed.reshape(-1), axis=0
    ).reshape(-1, width)
    kv = jnp.dot(
        chosen, kv_weight.reshape(width, 2 * local_width), preferred_element_type=jnp.float32
    ).astype(jnp.bfloat16)
    attended, query_grad, terms = attend(q, g, kv, allowed, live, heads)
    entries = lists.transpose(1, 0, 2, 3).reshape(-1)
    entry_rows = (entries[:, None] * KB + jnp.arange(KB)[None]).reshape(-1)
    onehot = (jnp.arange(key_count)[:, None] == entry_rows[None]).astype(jnp.bfloat16)
    weight_rows = width // (clip_count * audio_count)
    weight_grad, attended, query_grad = finish(
        terms,
        attended.reshape(frames, shard_rows, local_width),
        query_grad.reshape(frames, shard_rows, local_width),
        onehot,
        latents_all,
        (clip_count, frames, audio_count),
        weight_rows,
    )
    weight_grad = weight_grad.transpose(1, 0, 2).reshape(weight_rows, 2, local_width)
    return (attended[None], query_grad[None], weight_grad)


def solution(mesh):
    return jax.shard_map(
        per_device,
        mesh=mesh,
        in_specs=(
            P("dp", ("frame", "audio"), None),
            P("dp", ("frame", "audio"), None),
            P("dp", "audio", None),
            P(None, None, "frame"),
            P("dp"),
            P("dp"),
            P("dp", None, None),
        ),
        out_specs=(
            P("dp", ("frame", "audio"), None),
            P("dp", ("frame", "audio"), None),
            P(("dp", "audio"), None, "frame"),
        ),
        check_vma=False,
    )
```

```python
import functools
import math

import jax
import jax.numpy as jnp
from jax import lax
from jax.experimental import pallas as pl
from jax.experimental.pallas import tpu as pltpu
from jax.sharding import PartitionSpec as P

HD = 128
QB = 128
KB = 64


def dot_nt(a, b):
    return lax.dot_general(a, b, (((1,), (1,)), ((), ())), preferred_element_type=jnp.float32)


def dot_tn(a, b):
    return lax.dot_general(a, b, (((0,), (0,)), ((), ())), preferred_element_type=jnp.float32)


def attend_kernel(heads, chunk, bias_ref, live_ref, q_ref, g_ref, kv_ref, out_ref, dq_ref, dkv_ref):
    scaling = HD ** (-0.5)
    width = heads * HD
    bias = bias_ref[0]
    live = live_ref[0]
    group = math.gcd(heads, 4)
    for first in range(0, heads, group):
        cols = [slice(h * HD, (h + 1) * HD) for h in range(first, first + group)]
        vcols = [slice(width + c.start, width + c.stop) for c in cols]
        q = [q_ref[:, c] for c in cols]
        g = [g_ref[:, c] for c in cols]
        k = [kv_ref[:, c] for c in cols]
        v = [kv_ref[:, c] for c in vcols]
        scores = [dot_nt(x, y) * scaling for x, y in zip(q, k)]
        dprob = [dot_nt(x, y) for x, y in zip(g, v)]
        scores = [jnp.where(bias > 0.0, x, -1e30) for x in scores]
        weights = [jnp.exp(x - jnp.max(x, axis=-1, keepdims=True)) for x in scores]
        prob = [x / jnp.sum(x, axis=-1, keepdims=True) for x in weights]
        prob = [jnp.where(live > 0.0, x, 0.0) for x in prob]
        low = [x.astype(jnp.bfloat16) for x in prob]
        row = [jnp.sum(x * y, axis=-1, keepdims=True) for x, y in zip(prob, dprob)]
        ds = [(x * (y - r)).astype(jnp.bfloat16) for x, y, r in zip(prob, dprob, row)]
        outs = [jnp.dot(x, y, preferred_element_type=jnp.float32) for x, y in zip(low, v)]
        dqs = [jnp.dot(x, y, preferred_element_type=jnp.float32) * scaling for x, y in zip(ds, k)]
        dks = [dot_tn(x, y) * scaling for x, y in zip(ds, q)]
        dvs = [dot_tn(x, y) for x, y in zip(low, g)]
        for c, out, dq in zip(cols, outs, dqs):
            out_ref[:, c] = out.astype(jnp.bfloat16)
            dq_ref[:, c] = dq.astype(jnp.bfloat16)
        for c, part in zip(cols + vcols, dks + dvs):
            high = part.astype(jnp.bfloat16)
            at, lane = divmod(c.start, chunk)
            dkv_ref[at, :, lane : lane + HD] = high
            dkv_ref[at, :, chunk + lane : chunk + lane + HD] = (
                part - high.astype(jnp.float32)
            ).astype(jnp.bfloat16)


def pick_kernel(slot_ref, block_ref, *refs):
    pieces, out_ref, sems = refs[:-2], refs[-2], refs[-1]
    count = slot_ref.shape[0]

    def copy(piece, e):
        at = pl.ds(pl.multiple_of(block_ref[e] * KB, KB), KB)
        return pltpu.make_async_copy(piece.at[at], out_ref.at[pl.ds(e * KB, KB)], sems.at[e])

    for e in range(count):
        for s, piece in enumerate(pieces):
            pl.when(slot_ref[e] == s)(functools.partial(lambda p, e: copy(p, e).start(), piece, e))
    for e in range(count):
        copy(pieces[0], e).wait()


def pick(slots, blocks, pieces):
    smem = pl.BlockSpec(memory_space=pltpu.SMEM)
    count = slots.shape[0]
    return pl.pallas_call(
        pick_kernel,
        in_specs=[smem, smem] + [pl.BlockSpec(memory_space=pl.ANY)] * len(pieces),
        out_specs=pl.BlockSpec(memory_space=pltpu.VMEM),
        out_shape=jax.ShapeDtypeStruct((count * KB, pieces[0].shape[1]), jnp.bfloat16),
        scratch_shapes=[pltpu.SemaphoreType.DMA((count,))],
    )(slots, blocks, *pieces)


def attend(queries, cotangent, kv, allowed, live, heads):
    blocks = allowed.shape[0]
    keys = kv.shape[0] // blocks
    width = heads * HD
    chunk = math.gcd(2 * width, 256)
    chunks = 2 * width // chunk
    row_spec = pl.BlockSpec((QB, width), lambda b: (b, 0))
    kv_spec = pl.BlockSpec((keys, 2 * width), lambda b: (b, 0))
    return pl.pallas_call(
        functools.partial(attend_kernel, heads, chunk),
        grid=(blocks,),
        in_specs=[
            pl.BlockSpec((1, 1, keys), lambda b: (b, 0, 0)),
            pl.BlockSpec((1, QB, 1), lambda b: (b, 0, 0)),
            row_spec,
            row_spec,
            kv_spec,
        ],
        out_specs=[row_spec, row_spec, pl.BlockSpec((chunks, keys, 2 * chunk), lambda b: (0, b, 0))],
        out_shape=[
            jax.ShapeDtypeStruct(queries.shape, jnp.bfloat16),
            jax.ShapeDtypeStruct(queries.shape, jnp.bfloat16),
            jax.ShapeDtypeStruct((chunks, kv.shape[0], 2 * chunk), jnp.bfloat16),
        ],
    )(allowed, live, queries, cotangent, kv)


MESH = pl.DeviceIdType.MESH


def grad_kernel(
    axes, chunk, terms_ref, att_ref, dq_ref, onehot_ref, own_piece, near_piece, far_piece, last_piece,
    out_ref, att_out, dq_out,
    latents_vmem, cols_t, gathered, kv_tile, partial, right_buf, left_buf,
    local_sem, own_sem, far_send, far_recv, near_send, near_recv, fwd_send, fwd_recv,
    right_send, right_recv, left_send, left_recv, ret_send, ret_recv,
):
    clips, frames, audio = axes
    z, f, a = lax.axis_index("dp"), lax.axis_index("frame"), lax.axis_index("audio")
    chunks = terms_ref.shape[0]
    rows = terms_ref.shape[1]
    weight_rows = out_ref.shape[1]
    key_count = onehot_ref.shape[0]
    lane = att_ref.shape[2]
    half = audio // 2
    far = lax.rem(a + half, audio)
    near = a + 1 - 2 * lax.rem(a, 2)
    far_near = lax.rem(near + half, audio)

    piece_rows = own_piece.shape[0]
    loads = [
        pltpu.make_async_copy(
            piece, latents_vmem.at[pl.ds(s * piece_rows, piece_rows)], local_sem.at[s])
        for s, piece in enumerate((own_piece, near_piece, far_piece, last_piece))
    ]
    for load in loads:
        load.start()

    barrier = pltpu.get_barrier_semaphore()

    def greet(where):
        pl.semaphore_signal(barrier, inc=1, device_id=where, device_id_type=MESH)

    greet({"audio": far})
    greet({"audio": near})
    for step in range(1, frames):
        greet({"frame": lax.rem(f + step, frames)})
    pl.when(z > 0)(lambda: greet({"dp": z - 1}))
    pl.when(z < clips - 1)(lambda: greet({"dp": z + 1}))
    ends = jnp.where(z > 0, 1, 0) + jnp.where(z < clips - 1, 1, 0)
    pl.semaphore_wait(barrier, 1 + frames + ends)

    def far_copy(c):
        return pltpu.make_async_remote_copy(
            src_ref=terms_ref.at[c], dst_ref=gathered.at[c, a], send_sem=far_send.at[c],
            recv_sem=far_recv.at[c], device_id={"audio": far}, device_id_type=MESH)

    def near_copy(c):
        return pltpu.make_async_remote_copy(
            src_ref=terms_ref.at[c], dst_ref=gathered.at[c, a], send_sem=near_send.at[c],
            recv_sem=near_recv.at[c], device_id={"audio": near}, device_id_type=MESH)

    def fwd_copy(c):
        return pltpu.make_async_remote_copy(
            src_ref=gathered.at[c, far], dst_ref=gathered.at[c, far], send_sem=fwd_send.at[c],
            recv_sem=fwd_recv.at[c], device_id={"audio": near}, device_id_type=MESH)

    def arrived(c, source, sem, peer):
        return pltpu.make_async_remote_copy(
            src_ref=terms_ref.at[c], dst_ref=gathered.at[c, source], send_sem=far_send.at[c],
            recv_sem=sem.at[c], device_id={"audio": peer}, device_id_type=MESH)

    def own_copy(c):
        return pltpu.make_async_copy(terms_ref.at[c], gathered.at[c, a], own_sem.at[c])

    def issue(c, carry):
        far_copy(c).start()
        near_copy(c).start()
        own_copy(c).start()
        return carry

    lax.fori_loop(0, chunks, issue, 0)

    def lanes(g):
        return pl.ds(pl.multiple_of(g * lane, 128), lane)

    def returns(step):
        other = lax.rem(f + step, frames)
        return [
            pltpu.make_async_remote_copy(
                src_ref=src.at[frames - step], dst_ref=dst.at[:, lanes(f)],
                send_sem=ret_send.at[which, step], recv_sem=ret_recv.at[which, step],
                device_id={"frame": other}, device_id_type=MESH)
            for which, (src, dst) in enumerate(((att_ref, att_out), (dq_ref, dq_out)))
        ]

    for step in range(1, frames):
        for copy in returns(step):
            copy.start()
    att_out[:, lanes(f)] = att_ref[0]
    dq_out[:, lanes(f)] = dq_ref[0]

    for load in loads:
        load.wait()
    width = latents_vmem.shape[1]

    def select(d, carry):
        first = (d * audio + a) * weight_rows
        at = lax.broadcasted_iota(jnp.int32, (weight_rows, width), 1)
        row = lax.broadcasted_iota(jnp.int32, (weight_rows, width), 0)
        pick = jnp.where(at == row + first, 1.0, 0.0).astype(jnp.bfloat16)
        cols_t[d] = dot_nt(pick, latents_vmem[...]).astype(jnp.bfloat16)
        return carry

    lax.fori_loop(0, clips, select, 0)

    tile = math.gcd(key_count, 256)

    def compute(c):
        own_copy(c).wait()
        arrived(c, far, far_recv, far).wait_recv()
        fwd_copy(c).start()
        arrived(c, near, near_recv, near).wait_recv()
        arrived(c, far_near, fwd_recv, near).wait_recv()

        def dedupe(t, carry):
            at = pl.ds(pl.multiple_of(t * tile, tile), tile)
            total = jnp.zeros((tile, chunk), jnp.float32)
            for source in range(audio):
                pick = onehot_ref[at, source * rows : (source + 1) * rows]
                total += jnp.dot(
                    pick, gathered[c, source, :, :chunk], preferred_element_type=jnp.float32)
                total += jnp.dot(
                    pick, gathered[c, source, :, chunk:], preferred_element_type=jnp.float32)
            kv_tile[at, :] = total.astype(jnp.bfloat16)
            return carry

        lax.fori_loop(0, key_count // tile, dedupe, 0)

        def multiply(d, carry):
            partial[c, d] = jnp.dot(
                cols_t[d], kv_tile[...], preferred_element_type=jnp.float32
            ) * (1.0 / clips)
            return carry

        lax.fori_loop(0, clips, multiply, 0)
        out_ref[c] = partial[c, z]

    def hop(buf, send, recv, c, d, where):
        return pltpu.make_async_remote_copy(
            src_ref=buf.at[c, d], dst_ref=buf.at[c, d], send_sem=send.at[c, d],
            recv_sem=recv.at[c, d], device_id={"dp": where}, device_id_type=MESH)

    def pass_on(c, forward):
        if forward:
            buf, send, recv, peer, source = right_buf, right_send, right_recv, z + 1, z - 1
            has_source = z > 0
        else:
            buf, send, recv, peer, source = left_buf, left_send, left_recv, z - 1, z + 1
            has_source = z < clips - 1
        for d in range(clips):
            @pl.when((d > z) if forward else (d < z))
            def _():
                @pl.when(has_source)
                def _():
                    hop(buf, send, recv, c, d, source).wait_recv()
                    buf[c, d] = (partial[c, d] + buf[c, d].astype(jnp.float32)).astype(jnp.bfloat16)

                @pl.when(jnp.logical_not(has_source))
                def _():
                    buf[c, d] = partial[c, d].astype(jnp.bfloat16)

                hop(buf, send, recv, c, d, peer).start()

        @pl.when(has_source)
        def _():
            hop(buf, send, recv, c, z, source).wait_recv()
            out_ref[c] += buf[c, z].astype(jnp.float32)

    def advance(i, carry):
        pl.when(i < chunks)(lambda: compute(i))
        for forward, lag in ((True, z), (False, clips - 1 - z)):
            c = i - lag

            @pl.when(jnp.logical_and(c >= 0, c < chunks))
            def _():
                pass_on(c, forward)

        return carry

    lax.fori_loop(0, chunks + clips - 1, advance, 0)

    def drain(c, carry):
        far_copy(c).wait_send()
        near_copy(c).wait_send()
        fwd_copy(c).wait_send()
        for d in range(clips):
            pl.when(d > z)(lambda: hop(right_buf, right_send, right_recv, c, d, z + 1).wait_send())
            pl.when(d < z)(lambda: hop(left_buf, left_send, left_recv, c, d, z - 1).wait_send())
        return carry

    lax.fori_loop(0, chunks, drain, 0)
    for step in range(1, frames):
        for copy in returns(step):
            copy.wait_send()
        source = lax.rem(f + frames - step, frames)
        for which, (src, dst) in enumerate(((att_ref, att_out), (dq_ref, dq_out))):
            pltpu.make_async_remote_copy(
                src_ref=src.at[0], dst_ref=dst.at[:, lanes(source)],
                send_sem=ret_send.at[which, step], recv_sem=ret_recv.at[which, step],
                device_id={"frame": source}, device_id_type=MESH).wait_recv()


def finish(terms, attended, query_grad, onehot, pieces, sizes, weight_rows):
    clips, frames, audio = sizes
    chunks, rows, pair = terms.shape
    chunk = pair // 2
    own_rows, lane = attended.shape[1], attended.shape[2]
    key_count = onehot.shape[0]
    vmem = pl.BlockSpec(memory_space=pltpu.VMEM)
    dma = pltpu.SemaphoreType.DMA
    line = (chunks, clips)
    kernel = functools.partial(grad_kernel, sizes, chunk)
    return pl.pallas_call(
        kernel,
        in_specs=[vmem] * 4 + [pl.BlockSpec(memory_space=pl.ANY)] * len(pieces),
        out_specs=[vmem] * 3,
        out_shape=[
            jax.ShapeDtypeStruct((chunks, weight_rows, chunk), jnp.float32),
            jax.ShapeDtypeStruct((own_rows, frames * lane), jnp.bfloat16),
            jax.ShapeDtypeStruct((own_rows, frames * lane), jnp.bfloat16),
        ],
        scratch_shapes=[
            pltpu.VMEM((key_count, pieces[0].shape[1]), jnp.bfloat16),
            pltpu.VMEM((clips, weight_rows, key_count), jnp.bfloat16),
            pltpu.VMEM((chunks, audio, rows, pair), jnp.bfloat16),
            pltpu.VMEM((key_count, chunk), jnp.bfloat16),
            pltpu.VMEM((chunks, clips, weight_rows, chunk), jnp.float32),
            pltpu.VMEM((chunks, clips, weight_rows, chunk), jnp.bfloat16),
            pltpu.VMEM((chunks, clips, weight_rows, chunk), jnp.bfloat16),
            dma((len(pieces),)), dma((chunks,)), dma((chunks,)), dma((chunks,)), dma((chunks,)),
            dma((chunks,)), dma((chunks,)), dma((chunks,)),
            dma(line), dma(line), dma(line), dma(line),
            dma((2, frames)), dma((2, frames)),
        ],
        compiler_params=pltpu.CompilerParams(
            collective_id=0, has_side_effects=True, vmem_limit_bytes=66_000_000),
    )(terms, attended, query_grad, onehot, *pieces)


def per_device(
    video_query, out_grad, audio_latents, kv_weight, video_length, audio_length, align_list
):
    frames = lax.axis_size("frame")
    audio_count = lax.axis_size("audio")
    clip_count = lax.axis_size("dp")
    audio_at = lax.axis_index("audio")
    queries, cotangent, latents = video_query[0], out_grad[0], audio_latents[0]
    shard_rows = queries.shape[0]
    width = queries.shape[1]
    local_width = kv_weight.shape[2]
    heads = local_width // HD
    video_live, audio_live, block_lists = video_length[0], audio_length[0], align_list[0]
    listed_count = block_lists.shape[1]
    own_blocks = shard_rows // QB

    def swap(x, flip):
        return lax.ppermute(x, "audio", [(i, i ^ flip) for i in range(audio_count)])

    half = audio_count // 2
    frame_at = lax.axis_index("frame")

    def exchange(x):
        parts = [lax.dynamic_slice_in_dim(x, frame_at * local_width, local_width, 1)]
        for step in range(1, frames):
            part = lax.dynamic_slice_in_dim(
                x, (frame_at + step) % frames * local_width, local_width, 1)
            parts.append(
                lax.ppermute(part, "frame", [(i, (i + step) % frames) for i in range(frames)]))
        return jnp.concatenate(parts, axis=0)

    far_piece = swap(latents, half)
    near_piece = swap(latents, 1)
    q, g = exchange(queries), exchange(cotangent)
    weight = kv_weight.reshape(width, 2 * local_width)
    passed, weight = lax.optimization_barrier((far_piece, weight))
    pieces = [latents, near_piece, far_piece, swap(passed, 1)]
    piece_rows = latents.shape[0]
    key_count = audio_count * piece_rows
    turned = (frame_at - jnp.arange(frames)) % frames

    lists = block_lists.reshape(frames, audio_count, own_blocks, listed_count)[turned]
    listed = lax.dynamic_index_in_dim(lists, audio_at, 1, keepdims=False)
    listed = listed.reshape(frames * own_blocks, listed_count)
    block_at = (turned[:, None] * audio_count + audio_at) * own_blocks + jnp.arange(own_blocks)[None]
    block_at = block_at.reshape(-1)
    key_index = (listed[:, :, None] * KB + jnp.arange(KB)).reshape(
        frames * own_blocks, 1, listed_count * KB
    )
    allowed = (key_index < audio_live).astype(jnp.float32)
    row_index = block_at[:, None] * QB + jnp.arange(QB)[None]
    live = (row_index < video_live).astype(jnp.float32)[:, :, None]

    flat = listed.reshape(-1)
    piece_blocks = piece_rows // KB
    chosen = pick((flat // piece_blocks) ^ audio_at, flat % piece_blocks, pieces)
    kv = jnp.dot(
        chosen, weight, preferred_element_type=jnp.float32
    ).astype(jnp.bfloat16)
    attended, query_grad, terms = attend(q, g, kv, allowed, live, heads)
    entries = lists.transpose(1, 0, 2, 3).reshape(-1)
    entry_rows = (entries[:, None] * KB + jnp.arange(KB)[None]).reshape(-1)
    held = jnp.arange(key_count)
    held = ((held // piece_rows) ^ audio_at) * piece_rows + held % piece_rows
    onehot = (held[:, None] == entry_rows[None]).astype(jnp.bfloat16)
    weight_rows = width // (clip_count * audio_count)
    weight_grad, attended, query_grad = finish(
        terms,
        attended.reshape(frames, shard_rows, local_width),
        query_grad.reshape(frames, shard_rows, local_width),
        onehot,
        pieces,
        (clip_count, frames, audio_count),
        weight_rows,
    )
    weight_grad = weight_grad.transpose(1, 0, 2).reshape(weight_rows, 2, local_width)
    return (attended[None], query_grad[None], weight_grad)


def solution(mesh):
    return jax.shard_map(
        per_device,
        mesh=mesh,
        in_specs=(
            P("dp", ("frame", "audio"), None),
            P("dp", ("frame", "audio"), None),
            P("dp", "audio", None),
            P(None, None, "frame"),
            P("dp"),
            P("dp"),
            P("dp", None, None),
        ),
        out_specs=(
            P("dp", ("frame", "audio"), None),
            P("dp", ("frame", "audio"), None),
            P(("dp", "audio"), None, "frame"),
        ),
        check_vma=False,
    )
```

```python
import functools
import math

import jax
import jax.numpy as jnp
from jax import lax
from jax.experimental import pallas as pl
from jax.experimental.pallas import tpu as pltpu
from jax.sharding import PartitionSpec as P

HD = 128
QB = 128
KB = 64


def dot_nt(a, b):
    return lax.dot_general(a, b, (((1,), (1,)), ((), ())), preferred_element_type=jnp.float32)


def dot_tn(a, b):
    return lax.dot_general(a, b, (((0,), (0,)), ((), ())), preferred_element_type=jnp.float32)


def attend_kernel(heads, chunk, bias_ref, live_ref, q_ref, g_ref, kv_ref, out_ref, dq_ref, dkv_ref):
    scaling = HD ** (-0.5)
    width = heads * HD
    bias = bias_ref[0]
    live = live_ref[0]
    group = math.gcd(heads, 4)
    for first in range(0, heads, group):
        cols = [slice(h * HD, (h + 1) * HD) for h in range(first, first + group)]
        vcols = [slice(width + c.start, width + c.stop) for c in cols]
        q = [q_ref[:, c] for c in cols]
        g = [g_ref[:, c] for c in cols]
        k = [kv_ref[:, c] for c in cols]
        v = [kv_ref[:, c] for c in vcols]
        scores = [dot_nt(x, y) * scaling for x, y in zip(q, k)]
        dprob = [dot_nt(x, y) for x, y in zip(g, v)]
        scores = [jnp.where(bias > 0.0, x, -1e30) for x in scores]
        weights = [jnp.exp(x - jnp.max(x, axis=-1, keepdims=True)) for x in scores]
        prob = [x / jnp.sum(x, axis=-1, keepdims=True) for x in weights]
        prob = [jnp.where(live > 0.0, x, 0.0) for x in prob]
        low = [x.astype(jnp.bfloat16) for x in prob]
        row = [jnp.sum(x * y, axis=-1, keepdims=True) for x, y in zip(prob, dprob)]
        ds = [(x * (y - r)).astype(jnp.bfloat16) for x, y, r in zip(prob, dprob, row)]
        outs = [jnp.dot(x, y, preferred_element_type=jnp.float32) for x, y in zip(low, v)]
        dqs = [jnp.dot(x, y, preferred_element_type=jnp.float32) * scaling for x, y in zip(ds, k)]
        dks = [dot_tn(x, y) * scaling for x, y in zip(ds, q)]
        dvs = [dot_tn(x, y) for x, y in zip(low, g)]
        for c, out, dq in zip(cols, outs, dqs):
            out_ref[:, c] = out.astype(jnp.bfloat16)
            dq_ref[:, c] = dq.astype(jnp.bfloat16)
        for c, part in zip(cols + vcols, dks + dvs):
            high = part.astype(jnp.bfloat16)
            at, lane = divmod(c.start, chunk)
            dkv_ref[at, :, lane : lane + HD] = high
            dkv_ref[at, :, chunk + lane : chunk + lane + HD] = (
                part - high.astype(jnp.float32)
            ).astype(jnp.bfloat16)


def pick_kernel(slot_ref, block_ref, *refs):
    pieces, out_ref, sems = refs[:-2], refs[-2], refs[-1]
    count = slot_ref.shape[0]

    def copy(piece, e):
        at = pl.ds(pl.multiple_of(block_ref[e] * KB, KB), KB)
        return pltpu.make_async_copy(piece.at[at], out_ref.at[pl.ds(e * KB, KB)], sems.at[e])

    for e in range(count):
        for s, piece in enumerate(pieces):
            pl.when(slot_ref[e] == s)(functools.partial(lambda p, e: copy(p, e).start(), piece, e))
    for e in range(count):
        copy(pieces[0], e).wait()


def pick(slots, blocks, pieces):
    smem = pl.BlockSpec(memory_space=pltpu.SMEM)
    count = slots.shape[0]
    return pl.pallas_call(
        pick_kernel,
        in_specs=[smem, smem] + [pl.BlockSpec(memory_space=pl.ANY)] * len(pieces),
        out_specs=pl.BlockSpec(memory_space=pltpu.VMEM),
        out_shape=jax.ShapeDtypeStruct((count * KB, pieces[0].shape[1]), jnp.bfloat16),
        scratch_shapes=[pltpu.SemaphoreType.DMA((count,))],
    )(slots, blocks, *pieces)


def attend(queries, cotangent, kv, allowed, live, heads):
    blocks = allowed.shape[0]
    keys = kv.shape[0] // blocks
    width = heads * HD
    chunk = math.gcd(2 * width, 256)
    chunks = 2 * width // chunk
    row_spec = pl.BlockSpec((QB, width), lambda b: (b, 0))
    kv_spec = pl.BlockSpec((keys, 2 * width), lambda b: (b, 0))
    return pl.pallas_call(
        functools.partial(attend_kernel, heads, chunk),
        grid=(blocks,),
        in_specs=[
            pl.BlockSpec((1, 1, keys), lambda b: (b, 0, 0)),
            pl.BlockSpec((1, QB, 1), lambda b: (b, 0, 0)),
            row_spec,
            row_spec,
            kv_spec,
        ],
        out_specs=[row_spec, row_spec, pl.BlockSpec((chunks, keys, 2 * chunk), lambda b: (0, b, 0))],
        out_shape=[
            jax.ShapeDtypeStruct(queries.shape, jnp.bfloat16),
            jax.ShapeDtypeStruct(queries.shape, jnp.bfloat16),
            jax.ShapeDtypeStruct((chunks, kv.shape[0], 2 * chunk), jnp.bfloat16),
        ],
    )(allowed, live, queries, cotangent, kv)


MESH = pl.DeviceIdType.MESH


def grad_kernel(
    axes, chunk, terms_ref, att_ref, dq_ref, onehot_ref, own_piece, near_piece, far_piece, last_piece,
    out_ref, att_out, dq_out,
    latents_vmem, cols_t, gathered, kv_tile, partial, right_buf, left_buf,
    local_sem, own_sem, far_send, far_recv, near_send, near_recv, fwd_send, fwd_recv,
    right_send, right_recv, left_send, left_recv, ret_send, ret_recv,
):
    clips, frames, audio = axes
    z, f, a = lax.axis_index("dp"), lax.axis_index("frame"), lax.axis_index("audio")
    chunks = terms_ref.shape[0]
    rows = terms_ref.shape[1]
    weight_rows = out_ref.shape[1]
    key_count = onehot_ref.shape[0]
    lane = att_ref.shape[2]
    half = audio // 2
    far = lax.rem(a + half, audio)
    near = a + 1 - 2 * lax.rem(a, 2)
    far_near = lax.rem(near + half, audio)

    piece_rows = own_piece.shape[0]
    loads = [
        pltpu.make_async_copy(
            piece, latents_vmem.at[pl.ds(s * piece_rows, piece_rows)], local_sem.at[s])
        for s, piece in enumerate((own_piece, near_piece, far_piece, last_piece))
    ]
    for load in loads:
        load.start()

    barrier = pltpu.get_barrier_semaphore()

    def greet(where):
        pl.semaphore_signal(barrier, inc=1, device_id=where, device_id_type=MESH)

    greet({"audio": far})
    greet({"audio": near})
    for step in range(1, frames):
        greet({"frame": lax.rem(f + step, frames)})
    pl.when(z > 0)(lambda: greet({"dp": z - 1}))
    pl.when(z < clips - 1)(lambda: greet({"dp": z + 1}))
    ends = jnp.where(z > 0, 1, 0) + jnp.where(z < clips - 1, 1, 0)
    pl.semaphore_wait(barrier, 1 + frames + ends)

    def far_copy(c):
        return pltpu.make_async_remote_copy(
            src_ref=terms_ref.at[c], dst_ref=gathered.at[c, a], send_sem=far_send.at[c],
            recv_sem=far_recv.at[c], device_id={"audio": far}, device_id_type=MESH)

    def near_copy(c):
        return pltpu.make_async_remote_copy(
            src_ref=terms_ref.at[c], dst_ref=gathered.at[c, a], send_sem=near_send.at[c],
            recv_sem=near_recv.at[c], device_id={"audio": near}, device_id_type=MESH)

    def fwd_copy(c):
        return pltpu.make_async_remote_copy(
            src_ref=gathered.at[c, far], dst_ref=gathered.at[c, far], send_sem=fwd_send.at[c],
            recv_sem=fwd_recv.at[c], device_id={"audio": near}, device_id_type=MESH)

    def arrived(c, source, sem, peer):
        return pltpu.make_async_remote_copy(
            src_ref=terms_ref.at[c], dst_ref=gathered.at[c, source], send_sem=far_send.at[c],
            recv_sem=sem.at[c], device_id={"audio": peer}, device_id_type=MESH)

    def own_copy(c):
        return pltpu.make_async_copy(terms_ref.at[c], gathered.at[c, a], own_sem.at[c])

    def issue(c, carry):
        far_copy(c).start()
        near_copy(c).start()
        own_copy(c).start()
        return carry

    lax.fori_loop(0, chunks, issue, 0)

    def lanes(g):
        return pl.ds(pl.multiple_of(g * lane, 128), lane)

    def returns(step):
        other = lax.rem(f + step, frames)
        return [
            pltpu.make_async_remote_copy(
                src_ref=src.at[frames - step], dst_ref=dst.at[:, lanes(f)],
                send_sem=ret_send.at[which, step], recv_sem=ret_recv.at[which, step],
                device_id={"frame": other}, device_id_type=MESH)
            for which, (src, dst) in enumerate(((att_ref, att_out), (dq_ref, dq_out)))
        ]

    for step in range(1, frames):
        for copy in returns(step):
            copy.start()
    att_out[:, lanes(f)] = att_ref[0]
    dq_out[:, lanes(f)] = dq_ref[0]

    for load in loads:
        load.wait()
    width = latents_vmem.shape[1]

    def select(d, carry):
        first = (d * audio + a) * weight_rows
        at = lax.broadcasted_iota(jnp.int32, (weight_rows, width), 1)
        row = lax.broadcasted_iota(jnp.int32, (weight_rows, width), 0)
        pick = jnp.where(at == row + first, 1.0, 0.0).astype(jnp.bfloat16)
        cols_t[d] = dot_nt(pick, latents_vmem[...]).astype(jnp.bfloat16)
        return carry

    lax.fori_loop(0, clips, select, 0)

    tile = math.gcd(key_count, 256)

    def compute(c):
        own_copy(c).wait()
        arrived(c, far, far_recv, far).wait_recv()
        fwd_copy(c).start()
        arrived(c, near, near_recv, near).wait_recv()
        arrived(c, far_near, fwd_recv, near).wait_recv()

        def dedupe(t, carry):
            at = pl.ds(pl.multiple_of(t * tile, tile), tile)
            total = jnp.zeros((tile, chunk), jnp.float32)
            for source in range(audio):
                pick = onehot_ref[at, source * rows : (source + 1) * rows]
                total += jnp.dot(
                    pick, gathered[c, source, :, :chunk], preferred_element_type=jnp.float32)
                total += jnp.dot(
                    pick, gathered[c, source, :, chunk:], preferred_element_type=jnp.float32)
            kv_tile[at, :] = total.astype(jnp.bfloat16)
            return carry

        lax.fori_loop(0, key_count // tile, dedupe, 0)

        def multiply(d, carry):
            partial[c, d] = jnp.dot(
                cols_t[d], kv_tile[...], preferred_element_type=jnp.float32
            ) * (1.0 / clips)
            return carry

        lax.fori_loop(0, clips, multiply, 0)
        out_ref[c] = partial[c, z]

    def hop(buf, send, recv, c, d, where):
        return pltpu.make_async_remote_copy(
            src_ref=buf.at[c, d], dst_ref=buf.at[c, d], send_sem=send.at[c, d],
            recv_sem=recv.at[c, d], device_id={"dp": where}, device_id_type=MESH)

    def pass_on(c, forward):
        if forward:
            buf, send, recv, peer, source = right_buf, right_send, right_recv, z + 1, z - 1
            has_source = z > 0
        else:
            buf, send, recv, peer, source = left_buf, left_send, left_recv, z - 1, z + 1
            has_source = z < clips - 1
        for d in range(clips):
            @pl.when((d > z) if forward else (d < z))
            def _():
                @pl.when(has_source)
                def _():
                    hop(buf, send, recv, c, d, source).wait_recv()
                    buf[c, d] = (partial[c, d] + buf[c, d].astype(jnp.float32)).astype(jnp.bfloat16)

                @pl.when(jnp.logical_not(has_source))
                def _():
                    buf[c, d] = partial[c, d].astype(jnp.bfloat16)

                hop(buf, send, recv, c, d, peer).start()

        @pl.when(has_source)
        def _():
            hop(buf, send, recv, c, z, source).wait_recv()
            out_ref[c] += buf[c, z].astype(jnp.float32)

    def advance(i, carry):
        pl.when(i < chunks)(lambda: compute(i))
        for forward, lag in ((True, z), (False, clips - 1 - z)):
            c = i - lag

            @pl.when(jnp.logical_and(c >= 0, c < chunks))
            def _():
                pass_on(c, forward)

        return carry

    lax.fori_loop(0, chunks + clips - 1, advance, 0)

    def drain(c, carry):
        far_copy(c).wait_send()
        near_copy(c).wait_send()
        fwd_copy(c).wait_send()
        for d in range(clips):
            pl.when(d > z)(lambda: hop(right_buf, right_send, right_recv, c, d, z + 1).wait_send())
            pl.when(d < z)(lambda: hop(left_buf, left_send, left_recv, c, d, z - 1).wait_send())
        return carry

    lax.fori_loop(0, chunks, drain, 0)
    for step in range(1, frames):
        for copy in returns(step):
            copy.wait_send()
        source = lax.rem(f + frames - step, frames)
        for which, (src, dst) in enumerate(((att_ref, att_out), (dq_ref, dq_out))):
            pltpu.make_async_remote_copy(
                src_ref=src.at[0], dst_ref=dst.at[:, lanes(source)],
                send_sem=ret_send.at[which, step], recv_sem=ret_recv.at[which, step],
                device_id={"frame": source}, device_id_type=MESH).wait_recv()


def finish(terms, attended, query_grad, onehot, pieces, sizes, weight_rows):
    clips, frames, audio = sizes
    chunks, rows, pair = terms.shape
    chunk = pair // 2
    own_rows, lane = attended.shape[1], attended.shape[2]
    key_count = onehot.shape[0]
    vmem = pl.BlockSpec(memory_space=pltpu.VMEM)
    dma = pltpu.SemaphoreType.DMA
    line = (chunks, clips)
    kernel = functools.partial(grad_kernel, sizes, chunk)
    return pl.pallas_call(
        kernel,
        in_specs=[vmem] * 4 + [pl.BlockSpec(memory_space=pl.ANY)] * len(pieces),
        out_specs=[vmem] * 3,
        out_shape=[
            jax.ShapeDtypeStruct((chunks, weight_rows, chunk), jnp.float32),
            jax.ShapeDtypeStruct((own_rows, frames * lane), jnp.bfloat16),
            jax.ShapeDtypeStruct((own_rows, frames * lane), jnp.bfloat16),
        ],
        scratch_shapes=[
            pltpu.VMEM((key_count, pieces[0].shape[1]), jnp.bfloat16),
            pltpu.VMEM((clips, weight_rows, key_count), jnp.bfloat16),
            pltpu.VMEM((chunks, audio, rows, pair), jnp.bfloat16),
            pltpu.VMEM((key_count, chunk), jnp.bfloat16),
            pltpu.VMEM((chunks, clips, weight_rows, chunk), jnp.float32),
            pltpu.VMEM((chunks, clips, weight_rows, chunk), jnp.bfloat16),
            pltpu.VMEM((chunks, clips, weight_rows, chunk), jnp.bfloat16),
            dma((len(pieces),)), dma((chunks,)), dma((chunks,)), dma((chunks,)), dma((chunks,)),
            dma((chunks,)), dma((chunks,)), dma((chunks,)),
            dma(line), dma(line), dma(line), dma(line),
            dma((2, frames)), dma((2, frames)),
        ],
        compiler_params=pltpu.CompilerParams(
            collective_id=0, has_side_effects=True, vmem_limit_bytes=66_000_000),
    )(terms, attended, query_grad, onehot, *pieces)


def per_device(
    video_query, out_grad, audio_latents, kv_weight, video_length, audio_length, align_list
):
    frames = lax.axis_size("frame")
    audio_count = lax.axis_size("audio")
    clip_count = lax.axis_size("dp")
    audio_at = lax.axis_index("audio")
    queries, cotangent, latents = video_query[0], out_grad[0], audio_latents[0]
    shard_rows = queries.shape[0]
    width = queries.shape[1]
    local_width = kv_weight.shape[2]
    heads = local_width // HD
    video_live, audio_live, block_lists = video_length[0], audio_length[0], align_list[0]
    listed_count = block_lists.shape[1]
    own_blocks = shard_rows // QB

    def swap(x, flip):
        return lax.ppermute(x, "audio", [(i, i ^ flip) for i in range(audio_count)])

    half = audio_count // 2
    frame_at = lax.axis_index("frame")

    def exchange(x):
        parts = [lax.dynamic_slice_in_dim(x, frame_at * local_width, local_width, 1)]
        for step in range(1, frames):
            part = lax.dynamic_slice_in_dim(
                x, (frame_at + step) % frames * local_width, local_width, 1)
            parts.append(
                lax.ppermute(part, "frame", [(i, (i + step) % frames) for i in range(frames)]))
        return jnp.concatenate(parts, axis=0)

    far_piece = swap(latents, half)
    near_piece = swap(latents, 1)
    q, g = exchange(queries), exchange(cotangent)
    weight = kv_weight.reshape(width, 2 * local_width)
    piece_rows = latents.shape[0]
    key_count = audio_count * piece_rows
    turned = (frame_at - jnp.arange(frames)) % frames

    lists = block_lists.reshape(frames, audio_count, own_blocks, listed_count)[turned]
    listed = lax.dynamic_index_in_dim(lists, audio_at, 1, keepdims=False)
    listed = listed.reshape(frames * own_blocks, listed_count)
    block_at = (turned[:, None] * audio_count + audio_at) * own_blocks + jnp.arange(own_blocks)[None]
    block_at = block_at.reshape(-1)
    key_index = (listed[:, :, None] * KB + jnp.arange(KB)).reshape(
        frames * own_blocks, 1, listed_count * KB
    )
    allowed = (key_index < audio_live).astype(jnp.float32)
    row_index = block_at[:, None] * QB + jnp.arange(QB)[None]
    live = (row_index < video_live).astype(jnp.float32)[:, :, None]

    flat = listed.reshape(-1)
    piece_blocks = piece_rows // KB
    slots, blocks = (flat // piece_blocks) ^ audio_at, flat % piece_blocks
    passed, weight, q, g, slots, blocks, allowed = lax.optimization_barrier(
        (far_piece, weight, q, g, slots, blocks, allowed))
    pieces = [latents, near_piece, far_piece, swap(passed, 1)]
    chosen = pick(slots, blocks, pieces)
    kv = jnp.dot(
        chosen, weight, preferred_element_type=jnp.float32
    ).astype(jnp.bfloat16)
    attended, query_grad, terms = attend(q, g, kv, allowed, live, heads)
    entries = lists.transpose(1, 0, 2, 3).reshape(-1)
    entry_rows = (entries[:, None] * KB + jnp.arange(KB)[None]).reshape(-1)
    held = jnp.arange(key_count)
    held = ((held // piece_rows) ^ audio_at) * piece_rows + held % piece_rows
    onehot = (held[:, None] == entry_rows[None]).astype(jnp.bfloat16)
    weight_rows = width // (clip_count * audio_count)
    weight_grad, attended, query_grad = finish(
        terms,
        attended.reshape(frames, shard_rows, local_width),
        query_grad.reshape(frames, shard_rows, local_width),
        onehot,
        pieces,
        (clip_count, frames, audio_count),
        weight_rows,
    )
    weight_grad = weight_grad.transpose(1, 0, 2).reshape(weight_rows, 2, local_width)
    return (attended[None], query_grad[None], weight_grad)


def solution(mesh):
    return jax.shard_map(
        per_device,
        mesh=mesh,
        in_specs=(
            P("dp", ("frame", "audio"), None),
            P("dp", ("frame", "audio"), None),
            P("dp", "audio", None),
            P(None, None, "frame"),
            P("dp"),
            P("dp"),
            P("dp", None, None),
        ),
        out_specs=(
            P("dp", ("frame", "audio"), None),
            P("dp", ("frame", "audio"), None),
            P(("dp", "audio"), None, "frame"),
        ),
        check_vma=False,
    )
```
